32 devices in a mesh: seq: 8 (over z, y), section: 4 (over x, core).
Axes of the slice: x: 2, y: 2, z: 4, core: 2. Of those that a mesh axis runs over, the one named last changes fastest.
Arguments:
- queries: bfloat16 [4, 1024, 2048], P('section', 'seq'), may hold values from -6 to 6
- key_vectors: bfloat16 [4, 1024, 2048], P('section', 'seq'), may hold values from -6 to 6
- value_vectors: bfloat16 [4, 1024, 2048], P('section', 'seq'), may hold values from -6 to 6
- log_decay: bfloat16 [4, 1024, 2048], P('section', 'seq'), may hold values from -0.7 to 0, as said below
- write_strength: float32 [4, 16, 1024], P('section', None, 'seq'), may hold values from 0.1 to 0.9
- out_gain: float32 [4, 2048], P('section'), may hold values from 0.1 to 1.9
- out_weight: bfloat16 [4, 2048, 2304], P('section', None, 'seq'), may hold values from -0.125 to 0.125
Outputs:
- next_input: bfloat16 [4, 1024, 2304], P('section', 'seq')
The draws below stay inside these ranges and needn't reach their ends.
Inputs may be any that keep to these rules, and one draw needn't show every extreme that they name: `log_decay`: every entry is negative.
All inputs are finite; a program needn't handle non-finite values.
Results may differ from the reference program's by a relative error of at most 0.0051.
Values may be sent and summed in bfloat16 or wider, within the bound.
No kernel may reach another device: no remote copies, remote signals or barrier semaphores. Data moves between devices by JAX's collectives and lax.ppermute only.
A program may use at most 192 MiB of HBM per device.

```python
import math
import jax
import jax.numpy as jnp
from jax import lax

D = 2304
DK = 128
LOCAL_HEADS = 16
GROUP = 64
TOK_DEV = 128
HK = 2048
TOKENS = 1024
N_SECTION = 4


def draw_log_decay(key, part):
    key_kind, key_fast, key_slow, key_device, key_rough, key_place, key_dimension = jax.random.split(key, 7)
    share_fast = 0.4
    fast_head = (jax.random.uniform(key_kind, (N_SECTION, 1, 1, LOCAL_HEADS, 1)) < share_fast).astype(jnp.float32)
    fast_rate = jnp.exp(jax.random.uniform(key_fast, (N_SECTION, 1, 1, LOCAL_HEADS, DK), minval=math.log(1.0 / 50.0), maxval=math.log(1.0 / 30.0)))
    slow_rate = jnp.exp(jax.random.uniform(key_slow, (N_SECTION, 1, 1, LOCAL_HEADS, DK), minval=math.log(0.1), maxval=math.log(0.5))) / TOKENS
    base_rate = fast_head * fast_rate + (1.0 - fast_head) * slow_rate
    device_factor = jnp.exp(jax.random.uniform(key_device, (N_SECTION, TOKENS // TOK_DEV, 1, LOCAL_HEADS, 1), minval=math.log(0.6), maxval=math.log(1.5)))
    roughness = jax.random.uniform(key_rough, (N_SECTION, TOKENS // TOK_DEV, TOK_DEV, LOCAL_HEADS, DK), minval=0.5, maxval=1.5)
    constant_level = (base_rate * device_factor * roughness).reshape(N_SECTION, TOKENS, LOCAL_HEADS, DK)
    token_locations = jax.random.randint(key_place, (N_SECTION, 1, LOCAL_HEADS, 2), 0, TOKENS)
    sudden_sizes = jax.random.uniform(key_dimension, (N_SECTION, 1, LOCAL_HEADS, 2), minval=0.22, maxval=0.6)
    token_positions = lax.broadcasted_iota(jnp.int32, (1, TOKENS, 1, 1), 1)
    sudden_drop_loss = jnp.sum(jnp.where(token_positions == token_locations, sudden_sizes, 0.0), axis=-1)
    decay_logarithms = -(constant_level + sudden_drop_loss[..., None])
    return decay_logarithms.reshape(N_SECTION, TOKENS, LOCAL_HEADS * DK).astype(jnp.bfloat16)


def steps_of(key, extent, cuts, low, largest):
    def one(axis_at, parts):
        steps = jax.random.uniform(jax.random.fold_in(jax.random.fold_in(key, 6), axis_at), (parts,), jnp.float32, low / len(cuts), largest / len(cuts))
        return jnp.repeat(jnp.exp(steps), extent[axis_at] // parts).reshape((-1,) + (1,) * (len(extent) - axis_at - 1))

    level = one(*cuts[0])
    for cut in cuts[1:]:
        level = level * one(*cut)
    return level


def normal_values(key, dims, width, reach, cuts=(), held_as=jnp.bfloat16):
    factor_of = steps_of(key, dims, cuts, -0.22, 0.18) if cuts else 1.0
    values = jax.random.normal(key, dims, jnp.float32) * width * factor_of
    return jnp.minimum(jnp.maximum(values, -reach), reach).astype(held_as)


def setup_inputs(seed: int = 0) -> dict:
    splits = jax.random.split(jax.random.key(seed), 8)
    return {
        "queries": normal_values(splits[0], (N_SECTION, TOKENS, HK), 1.0, 6.0, ((0, 4), (1, 8))),
        "key_vectors": normal_values(splits[1], (N_SECTION, TOKENS, HK), 1.0, 6.0, ((0, 4), (1, 8))),
        "value_vectors": normal_values(splits[2], (N_SECTION, TOKENS, HK), 1.0, 6.0, ((0, 4), (1, 8))),
        "log_decay": draw_log_decay(jax.random.fold_in(splits[7], 71), 0),
        "write_strength": jnp.clip(0.1 + 0.79999997 * jax.random.uniform(splits[4], (N_SECTION, LOCAL_HEADS, TOKENS), jnp.float32) ** steps_of(splits[4], (N_SECTION, LOCAL_HEADS, TOKENS), ((0, 4), (2, 8)), -0.2, 0.2), 0.1, 0.9),
        "out_gain": jnp.clip(1.0 + 0.18 * jax.random.normal(splits[5], (N_SECTION, HK), jnp.float32), 0.1, 1.9),
        "out_weight": normal_values(splits[6], (N_SECTION, HK, D), HK ** -0.5, 0.125, ((0, 4), (2, 8))),
    }


exact_precision = lax.Precision.HIGHEST

def unit_rows(values):
    return values * lax.rsqrt(lax.optimization_barrier(jnp.sum(values * values, axis=-1, keepdims=True)) + 1e-06)

def prepare(query_block, key_unit, value_block, decay_block, strength):
    length = decay_block.shape[-2]
    cumulative = jnp.cumsum(decay_block, axis=-2)
    grown = jnp.exp(cumulative)
    shrunk = jnp.exp(-cumulative)
    end_decay = grown[..., -1:, :]
    key_grown = key_unit * grown
    key_shrunk = key_unit * shrunk
    query_grown = query_block * grown
    row_index = lax.broadcasted_iota(jnp.int32, (length, length), 0)
    col_index = lax.broadcasted_iota(jnp.int32, (length, length), 1)
    strict_lower = (row_index > col_index).astype(jnp.float32)
    with_diagonal = (row_index >= col_index).astype(jnp.float32)
    weight_row = strength[..., None, :]
    key_mix = jnp.einsum('...id,...jd->...ij', key_grown, key_shrunk, precision=exact_precision) * strict_lower * weight_row
    unit_lower = key_mix + jnp.eye(length, dtype=jnp.float32)
    solved_values = jax.scipy.linalg.solve_triangular(unit_lower, value_block, lower=True, unit_diagonal=True)
    solved_keys = jax.scipy.linalg.solve_triangular(unit_lower, key_grown, lower=True, unit_diagonal=True)
    query_mix = jnp.einsum('...id,...jd->...ij', query_grown, key_shrunk, precision=exact_precision) * with_diagonal * weight_row
    end_keys = key_shrunk * end_decay * strength[..., :, None]
    return (solved_values, solved_keys, query_grown, query_mix, end_keys, end_decay)

def advance(running_state, prepared):
    solved_values, solved_keys, query_grown, query_mix, end_keys, end_decay = prepared
    written = solved_values - jnp.einsum('hcd,hde->hce', solved_keys, running_state, precision=exact_precision)
    core_out = jnp.einsum('hcd,hde->hce', query_grown, running_state, precision=exact_precision)
    core_out = core_out + jnp.einsum('hij,hje->hie', query_mix, written, precision=exact_precision)
    running_state = end_decay[:, 0, :, None] * running_state + jnp.einsum('hcd,hce->hde', end_keys, written, precision=exact_precision)
    return (running_state, core_out)

def section_output(queries, key_vectors, value_vectors, log_decay, write_strength, out_gain, out_weight):
    group_count = queries.shape[0] // GROUP

    def to_heads(values):
        return values.astype(jnp.float32).reshape(group_count, GROUP, LOCAL_HEADS, DK).transpose(0, 2, 1, 3)
    query_block = to_heads(queries)
    key_unit = unit_rows(to_heads(key_vectors))
    value_block = to_heads(value_vectors)
    decay_block = to_heads(log_decay)
    strength = write_strength.reshape(LOCAL_HEADS, group_count, GROUP).transpose(1, 0, 2)

    def group_step(running_state, pieces):
        return advance(running_state, prepare(*pieces))
    start_state = jnp.zeros((LOCAL_HEADS, DK, DK), jnp.float32)
    _, cores = lax.scan(group_step, start_state, (query_block, key_unit, value_block, decay_block, strength))
    core_all = cores.transpose(0, 2, 1, 3).reshape(group_count * GROUP, LOCAL_HEADS, DK)
    inverse_rms = lax.rsqrt(lax.optimization_barrier(jnp.mean(core_all * core_all, axis=-1, keepdims=True)) + 1e-05)
    normed = (core_all * inverse_rms * out_gain.reshape(LOCAL_HEADS, DK)).reshape(group_count * GROUP, LOCAL_HEADS * DK).astype(jnp.bfloat16)
    return jnp.dot(normed.astype(jnp.float32), out_weight.astype(jnp.float32), preferred_element_type=jnp.float32).astype(jnp.bfloat16)

def reference(queries, key_vectors, value_vectors, log_decay, write_strength, out_gain, out_weight):
    mixers = []
    for section_number in range(N_SECTION):
        mixers.append(section_output(queries[section_number], key_vectors[section_number], value_vectors[section_number], log_decay[section_number], write_strength[section_number], out_gain[section_number], out_weight[section_number]))
    stacked = jnp.stack(mixers, axis=0)
    return jnp.concatenate([stacked[-1:], stacked[:-1]], axis=0)
```

```python
import functools

import jax
import jax.numpy as jnp
from jax import lax
from jax.experimental import pallas as pl
from jax.experimental.pallas import tpu as pltpu
from jax.sharding import PartitionSpec as P

F32 = jnp.float32
BF16 = jnp.bfloat16
QUAD = 4
VMEM_LIMIT = 48 << 20


def split(a):
    high = a.astype(BF16)
    return high, (a - high.astype(F32)).astype(BF16)


def dot1(a, b, dims=((1,), (0,))):
    return lax.dot_general(a, b, (dims, ((), ())), preferred_element_type=F32)


def dot3(a, b, dims=((1,), (0,))):
    return dot1(a[0], b[0], dims) + dot1(a[0], b[1], dims) + dot1(a[1], b[0], dims)


ROWS = ((1,), (1,))


def iotas(n):
    row = lax.broadcasted_iota(jnp.int32, (n, n), 0)
    col = lax.broadcasted_iota(jnp.int32, (n, n), 1)
    return row, col


def unit_lower_inverse(strict, row, col):
    n = strict.shape[0]
    inverse = (row == col).astype(F32)
    size = 1
    while size < n:
        shift = size.bit_length() - 1
        joins = ((row >> (shift + 1)) == (col >> (shift + 1))) & ((row >> shift) > (col >> shift))
        below = jnp.where(joins, strict, 0.0)
        if size == 1:
            inverse = inverse - below
        else:
            parts = split(inverse)
            inverse = inverse - dot3(parts, split(dot3(split(below), parts)))
        size *= 2
    return inverse


def pick(pieces, rank):
    p = list(pieces)
    one = (rank & 1) == 1
    two = (rank & 2) == 2
    p = [jnp.where(one, p[x ^ 1], p[x]) for x in range(4)]
    return [jnp.where(two, p[x ^ 2], p[x]) for x in range(4)]


def pack_kl(rank_ref, k_ref, l_ref, b_ref, *outs):
    rank = rank_ref[0]
    tok = k_ref.shape[0]
    width = outs[0].shape[1]
    dk = 128
    heads = width // dk
    for x in range(4):
        owner = rank ^ x
        at = pl.multiple_of(owner * width, width)
        outs[x][0:tok, :] = k_ref[:, pl.ds(at, width)]
        outs[x][tok : 2 * tok, :] = l_ref[:, pl.ds(at, width)]
        for h in range(heads):
            strength = b_ref[pl.ds(owner * heads + h, 1), :]
            first, rest = split(strength)
            second, third = split(strength - first.astype(F32))
            rows = jnp.concatenate(
                [first.astype(F32), second.astype(F32), third.astype(F32), jnp.zeros((13, tok), F32)], axis=0
            )
            outs[x][2 * tok : 2 * tok + 16, h * dk : (h + 1) * dk] = rows.astype(BF16)


def pack_vq(rank_ref, v_ref, q_ref, *outs):
    rank = rank_ref[0]
    width = outs[0].shape[1]
    for x in range(4):
        at = pl.multiple_of((rank ^ x) * width, width)
        outs[x][...] = v_ref[:, pl.ds(at, width)]
        outs[4 + x][...] = q_ref[:, pl.ds(at, width)]


def decays(log_decay, row, col):
    cumulative = dot1((row >= col).astype(BF16), log_decay)
    n = cumulative.shape[0]
    middle = cumulative[n // 2 - 1 : n // 2, :]
    end = cumulative[n - 1 : n, :]
    return cumulative, middle, end


def states_kernel(rank_ref, *refs):
    kl = refs[0:4]
    v = refs[4:8]
    key_solved_ref, value_solved_ref, shrunk_ref, map_ref, state_ref, total_ref = refs[8:]
    rank = rank_ref[0]
    n = 128
    row, col = iotas(n)
    kl_c = pick([r[...] for r in kl], rank)
    v_c = pick([r[...] for r in v], rank)
    state = None
    for c in range(4):
        key = kl_c[c][0:n].astype(F32)
        log_decay = kl_c[c][n : 2 * n]
        bs = kl_c[c][2 * n : 2 * n + 16].astype(F32)
        strength = bs[0:1] + bs[1:2] + bs[2:3]
        strength_col = jnp.sum(jnp.where(row == col, strength, 0.0), axis=1, keepdims=True)
        key = key * lax.rsqrt(jnp.sum(key * key, axis=-1, keepdims=True) + 1e-06)
        cumulative, middle, end = decays(log_decay, row, col)
        grown = key * jnp.exp(cumulative - middle)
        shrunk = key * jnp.exp(middle - cumulative) * strength_col
        grown_s, shrunk_s = split(grown), split(shrunk)
        strict = jnp.where(row > col, dot3(grown_s, shrunk_s, ROWS), 0.0)
        inverse = split(unit_lower_inverse(strict, row, col))
        key_solved = dot3(inverse, grown_s) * jnp.exp(middle)
        value_solved = dot1(inverse[0], v_c[c]) + dot1(inverse[1], v_c[c])
        key_s, value_s = split(key_solved), split(value_solved)
        end_keys = split((shrunk * jnp.exp(end - middle)).T)
        end_col = jnp.sum(jnp.where(row == col, jnp.exp(end), 0.0), axis=1, keepdims=True)
        step = jnp.where(row == col, end_col, 0.0) - dot3(end_keys, key_s)
        offset = dot3(end_keys, value_s)
        key_solved_ref[0, c] = key_solved
        value_solved_ref[0, c] = value_solved
        shrunk_ref[0, c] = shrunk
        map_ref[0, c] = step
        if c == 0:
            state_ref[0, c] = jnp.zeros((n, n), F32)
            state = offset
        else:
            state_ref[0, c] = state
            state = dot3(split(step), split(state)) + offset
    total_ref[0] = state


def local_kernel(rank_ref, *refs):
    kl = refs[0:4]
    q = refs[4:8]
    key_solved_ref, value_solved_ref, shrunk_ref, state_ref, query_ref, core_ref = refs[8:]
    rank = rank_ref[0]
    n = 128
    row, col = iotas(n)
    l_c = pick([r[n : 2 * n] for r in kl], rank)
    q_c = pick([r[...] for r in q], rank)
    for c in range(4):
        cumulative, middle, end = decays(l_c[c], row, col)
        grown = q_c[c].astype(F32) * jnp.exp(cumulative - middle)
        mix = jnp.where(row >= col, dot3(split(grown), split(shrunk_ref[0, c]), ROWS), 0.0)
        mix_s = split(mix)
        query = grown * jnp.exp(middle) - dot3(mix_s, split(key_solved_ref[0, c]))
        core = dot3(mix_s, split(value_solved_ref[0, c]))
        if c > 0:
            core = core + dot3(split(query), split(state_ref[0, c]))
        query_ref[0, c] = query
        core_ref[0, c] = core


def finish_kernel(start_ref, map_ref, query_ref, core_ref, gain_ref, out_ref):
    state = start_ref[0].astype(F32)
    n = 128
    for c in range(4):
        state_s = split(state)
        core = core_ref[0, c] + dot3(split(query_ref[0, c]), state_s)
        if c < 3:
            state = dot3(split(map_ref[0, c]), state_s)
        scale = lax.rsqrt(jnp.mean(core * core, axis=-1, keepdims=True) + 1e-05)
        out_ref[c * n : (c + 1) * n, :] = (core * scale * gain_ref[...]).astype(BF16)


def per_device(q, k, v, l, strength, gain, weight):
    q, k, v, l, strength, gain, weight = (a[0] for a in (q, k, v, l, strength, gain, weight))
    tok, hk = q.shape
    heads = strength.shape[0]
    dk = hk // heads
    seq = lax.axis_size("seq")
    sections = lax.axis_size("section")
    groups = seq // QUAD
    width = hk // QUAD
    hq = heads // QUAD
    position = lax.axis_index("seq")
    rank = (position % QUAD).astype(jnp.int32)
    rank1 = rank.reshape(1)
    smem = pl.BlockSpec(memory_space=pltpu.SMEM)
    params = pltpu.CompilerParams(vmem_limit_bytes=VMEM_LIMIT)

    def call(kernel, name, **kw):
        return pl.pallas_call(kernel, name=name, compiler_params=params, **kw)

    def near(value, x):
        return lax.ppermute(value, "seq", [(i, i ^ x) for i in range(seq)])

    full = lambda shape: pl.BlockSpec(shape, lambda *_: (0,) * len(shape))
    kl = call(
        pack_kl,
        "pack_kl",
        grid=(1,),
        in_specs=[smem, full((tok, hk)), full((tok, hk)), full((heads, tok))],
        out_specs=[full((2 * tok + 16, width))] * 4,
        out_shape=[jax.ShapeDtypeStruct((2 * tok + 16, width), BF16)] * 4,
    )(rank1, k, l, strength)
    vq = call(
        pack_vq,
        "pack_vq",
        grid=(1,),
        in_specs=[smem, full((tok, hk)), full((tok, hk))],
        out_specs=[full((tok, width))] * 8,
        out_shape=[jax.ShapeDtypeStruct((tok, width), BF16)] * 8,
    )(rank1, v, q)
    kl = [kl[0]] + [near(kl[x], x) for x in range(1, 4)]
    vs = [vq[0]] + [near(vq[x], x) for x in range(1, 4)]
    qs = [vq[4]] + [near(vq[4 + x], x) for x in range(1, 4)]
    far_weights = [weight]
    for g in range(1, groups):
        far_weights.append(
            lax.ppermute(weight, "seq", [(i, (i + g * QUAD) % seq) for i in range(seq)])
        )

    kl_spec = pl.BlockSpec((2 * tok + 16, dk), lambda h: (0, h))
    x_spec = pl.BlockSpec((tok, dk), lambda h: (0, h))
    m_spec = pl.BlockSpec((1, QUAD, tok, dk), lambda h: (h, 0, 0, 0))
    m_shape = jax.ShapeDtypeStruct((hq, QUAD, tok, dk), F32)
    s_spec = pl.BlockSpec((1, dk, dk), lambda h: (h, 0, 0))
    key_solved, value_solved, shrunk, maps, states, total = call(
        states_kernel,
        "states",
        grid=(hq,),
        in_specs=[smem] + [kl_spec] * 4 + [x_spec] * 4,
        out_specs=[m_spec] * 5 + [s_spec],
        out_shape=[m_shape] * 5 + [jax.ShapeDtypeStruct((hq, dk, dk), F32)],
    )(rank1, *kl, *vs)

    onward = [(i, i + QUAD) for i in range(seq - QUAD)]
    start = lax.ppermute(total, "seq", onward)
    for _ in range(groups - 2):
        state = start
        for c in range(QUAD):
            state = jnp.einsum("hde,hef->hdf", maps[:, c], state, precision=lax.Precision.HIGHEST)
        start = lax.ppermute(state + total, "seq", onward)

    query, core = call(
        local_kernel,
        "local",
        grid=(hq,),
        in_specs=[smem] + [kl_spec] * 4 + [x_spec] * 4 + [m_spec] * 4,
        out_specs=[m_spec] * 2,
        out_shape=[m_shape] * 2,
    )(rank1, *kl, *qs, key_solved, value_solved, shrunk, states)
    gain_here = lax.dynamic_slice(gain.reshape(QUAD, 1, width), (rank, 0, 0), (1, 1, width))[0]
    normed = call(
        finish_kernel,
        "finish",
        grid=(hq,),
        in_specs=[s_spec, m_spec, m_spec, m_spec, pl.BlockSpec((1, dk), lambda h: (0, h))],
        out_specs=pl.BlockSpec((QUAD * tok, dk), lambda h: (0, h)),
        out_shape=jax.ShapeDtypeStruct((QUAD * tok, width), BF16),
    )(start, maps, query, core, gain_here)

    normed = [normed] + [near(normed, x) for x in range(1, 4)]

    def product_kernel(rank_ref, *refs):
        n_refs, w_refs, outs = refs[:4], refs[4 : 4 + groups], refs[4 + groups :]
        rank = rank_ref[0]
        cols = weight.shape[1]
        parts = []
        for w in w_refs:
            acc = None
            for x in range(4):
                at = pl.multiple_of((rank ^ x) * width, width)
                term = dot1(n_refs[x][...], w[pl.ds(at, width), :])
                acc = term if acc is None else acc + term
            parts.append(acc.astype(BF16))
        for c in range(4):
            for g in range(groups):
                outs[c][:, g * cols : (g + 1) * cols] = parts[g][c * tok : (c + 1) * tok]

    cols = weight.shape[1]
    pieces = call(
        product_kernel,
        "product",
        grid=(1,),
        in_specs=[smem] + [full((QUAD * tok, width))] * 4 + [full(weight.shape)] * groups,
        out_specs=[full((tok, groups * cols))] * 4,
        out_shape=[jax.ShapeDtypeStruct((tok, groups * cols), BF16)] * 4,
    )(rank1, *normed, *far_weights)

    sent = pick(pieces, rank)
    got = []
    for x in range(4):
        pairs = []
        for i in range(seq):
            for s in range(sections):
                pairs.append((i * sections + s, (i ^ x) * sections + (s + 1) % sections))
        got.append(lax.ppermute(sent[x], ("seq", "section"), pairs))
    by_rank = pick(got, rank)
    stack = jnp.stack(by_rank).reshape(QUAD, tok, groups, cols)
    group = position // QUAD
    columns = [
        lax.dynamic_index_in_dim(stack, (group - g) % groups, axis=2, keepdims=False)
        for g in range(groups)
    ]
    out = jnp.stack(columns)
    out = out.transpose(2, 0, 1, 3).reshape(tok, groups * QUAD * cols)
    return out[None]


def solution(mesh):
    in_specs = (
        P("section", "seq", None),
        P("section", "seq", None),
        P("section", "seq", None),
        P("section", "seq", None),
        P("section", None, "seq"),
        P("section", None),
        P("section", None, "seq"),
    )
    out_specs = P("section", "seq", None)
    return jax.shard_map(
        per_device, mesh=mesh, in_specs=in_specs, out_specs=out_specs, check_vma=False
    )
```

```python
import functools

import jax
import jax.numpy as jnp
from jax import lax
from jax.experimental import pallas as pl
from jax.experimental.pallas import tpu as pltpu
from jax.sharding import PartitionSpec as P

F32 = jnp.float32
BF16 = jnp.bfloat16
QUAD = 4
SHARES = (8,)
ROWS = ((1,), (1,))


def split(a):
    high = a.astype(BF16)
    return high, (a - high.astype(F32)).astype(BF16)


def store_split(ref, at, a):
    high, low = split(a)
    n = a.shape[1]
    ref[(*at, slice(None), slice(0, n))] = high
    ref[(*at, slice(None), slice(n, 2 * n))] = low


def load_split(ref, at):
    both = ref[at]
    n = both.shape[1] // 2
    return both[:, :n], both[:, n:]


def dot1(a, b, dims=((1,), (0,))):
    return lax.dot_general(a, b, (dims, ((), ())), preferred_element_type=F32)


def dot2(a, b, dims=((1,), (0,))):
    return dot1(a[0], b, dims) + dot1(a[1], b, dims)


def dot3(a, b, dims=((1,), (0,))):
    return dot1(a[0], b[0], dims) + dot1(a[0], b[1], dims) + dot1(a[1], b[0], dims)


def iotas(n):
    row = lax.broadcasted_iota(jnp.int32, (n, n), 0)
    col = lax.broadcasted_iota(jnp.int32, (n, n), 1)
    return row, col


def unit_lower_inverses(stricts, row, col):
    n = stricts[0].shape[0]
    eye = (row == col).astype(F32)
    inverses = None
    size = 1
    while size < n:
        shift = size.bit_length() - 1
        joins = ((row >> (shift + 1)) == (col >> (shift + 1))) & ((row >> shift) > (col >> shift))
        below = [jnp.where(joins, s, 0.0) for s in stricts]
        if size == 1:
            inverses = [eye - b for b in below]
        else:
            parts = [split(i) for i in inverses]
            inner = [split(dot3(split(b), p)) for b, p in zip(below, parts)]
            outer = [dot3(p, t) for p, t in zip(parts, inner)]
            inverses = [i - o for i, o in zip(inverses, outer)]
        size *= 2
    return inverses


def pick(pieces, rank):
    p = list(pieces)
    one = (rank & 1) == 1
    two = (rank & 2) == 2
    p = [jnp.where(one, p[x ^ 1], p[x]) for x in range(4)]
    return [jnp.where(two, p[x ^ 2], p[x]) for x in range(4)]


def pack_kl(tok, width, dk, rank_ref, k_ref, l_ref, b_ref, *refs):
    outs, sem = refs[:4], refs[4]
    rank = rank_ref[0]
    heads = width // dk
    copies = []
    for x in range(4):
        at = pl.multiple_of((rank ^ x) * width, width)
        for i, source in enumerate((k_ref, l_ref)):
            copy = pltpu.make_async_copy(
                source.at[:, pl.ds(at, width)], outs[x].at[i * tok : (i + 1) * tok, :], sem.at[2 * x + i]
            )
            copy.start()
            copies.append(copy)
    for x in range(4):
        for h in range(heads):
            strength = b_ref[pl.ds((rank ^ x) * heads + h, 1), :]
            first, rest = split(strength)
            second, third = split(strength - first.astype(F32))
            rows = jnp.concatenate(
                [first.astype(F32), second.astype(F32), third.astype(F32), jnp.zeros((13, tok), F32)], axis=0
            )
            outs[x][2 * tok : 2 * tok + 16, h * dk : (h + 1) * dk] = rows.astype(BF16)
    for copy in copies:
        copy.wait()


def pack_vq(tok, width, rank_ref, v_ref, q_ref, *refs):
    outs, sem = refs[:4], refs[4]
    rank = rank_ref[0]
    copies = []
    for x in range(4):
        at = pl.multiple_of((rank ^ x) * width, width)
        for i, source in enumerate((v_ref, q_ref)):
            copy = pltpu.make_async_copy(
                source.at[:, pl.ds(at, width)], outs[x].at[i * tok : (i + 1) * tok, :], sem.at[2 * x + i]
            )
            copy.start()
            copies.append(copy)
    for copy in copies:
        copy.wait()


def chunks_of(refs, rank, rows, nh, dk):
    out = []
    for h in range(nh):
        out += pick([r[rows, h * dk : (h + 1) * dk] for r in refs], rank)
    return out


def maps_kernel(nh, n, more, rank_ref, *refs):
    kl = refs[0:4]
    inverse_ref, offset_ref, key_ref, shrunk_ref, map_ref, before_ref = refs[4:10]
    rank = rank_ref[0]
    row, col = iotas(n)
    diag = row == col
    tri = (row >= col).astype(BF16)
    every = range(4 * nh)
    at = [(i // 4, i % 4) for i in every]
    bs = [b.astype(F32) for b in chunks_of(kl, rank, slice(2 * n, 2 * n + 16), nh, n)]
    bs = [b[0:1] + b[1:2] + b[2:3] for b in bs]
    strength = [jnp.sum(jnp.where(diag, b, 0.0), axis=1, keepdims=True) for b in bs]
    key = [k.astype(F32) for k in chunks_of(kl, rank, slice(0, n), nh, n)]
    key = [k * lax.rsqrt(jnp.sum(k * k, axis=-1, keepdims=True) + 1e-06) for k in key]
    cum = [dot1(tri, l) for l in chunks_of(kl, rank, slice(n, 2 * n), nh, n)]
    mid = [c[n // 2 - 1 : n // 2] for c in cum]
    end = [c[n - 1 : n] for c in cum]
    grown = [split(key[i] * jnp.exp(cum[i] - mid[i])) for i in every]
    shrunk = [key[i] * jnp.exp(mid[i] - cum[i]) * strength[i] for i in every]
    shrunk_s = [split(s) for s in shrunk]
    strict = [jnp.where(row > col, dot3(grown[i], shrunk_s[i], ROWS), 0.0) for i in every]
    inverse = [split(x) for x in unit_lower_inverses(strict, row, col)]
    solved = [split(dot3(inverse[i], grown[i]) * jnp.exp(mid[i])) for i in every]
    end_keys = [split((shrunk[i] * jnp.exp(end[i] - mid[i])).T) for i in every]
    end_col = [jnp.sum(jnp.where(diag, jnp.exp(e), 0.0), axis=1, keepdims=True) for e in end]
    step = [jnp.where(diag, end_col[i], 0.0) - dot3(end_keys[i], solved[i]) for i in every]
    step_s = [split(s) for s in step]
    for i in every:
        for ref, value in ((inverse_ref, inverse[i]), (key_ref, solved[i]), (shrunk_ref, shrunk_s[i]), (map_ref, step_s[i])):
            ref[(*at[i], slice(None), slice(0, n))] = value[0]
            ref[(*at[i], slice(None), slice(n, 2 * n))] = value[1]
        store_split(offset_ref, at[i], dot3(end_keys[i], inverse[i]))
    before = [step[4 * h] for h in range(nh)]
    for c in range(1, 4):
        for h in range(nh):
            store_split(before_ref, (h, c - 1), before[h])
            if c < 3 or more:
                before[h] = dot3(step_s[4 * h + c], split(before[h]))
    if more:
        for h in range(nh):
            refs[10][h] = before[h]


def states_kernel(nh, n, rank_ref, *refs):
    v = refs[0:4]
    offset_ref, map_ref, state_ref, total_ref = refs[4:]
    value = chunks_of(v, rank_ref[0], slice(0, n), nh, n)
    offset = [dot2(load_split(offset_ref, (i // 4, i % 4)), value[i]) for i in range(4 * nh)]
    state = [offset[4 * h] for h in range(nh)]
    for c in range(1, 4):
        parts = [split(s) for s in state]
        for h in range(nh):
            state_ref[h, c - 1, :, 0:n] = parts[h][0]
            state_ref[h, c - 1, :, n : 2 * n] = parts[h][1]
        state = [dot3(load_split(map_ref, (h, c)), parts[h]) + offset[4 * h + c] for h in range(nh)]
    for h in range(nh):
        total_ref[h] = state[h].astype(total_ref.dtype)


def local_kernel(nh, n, rank_ref, *refs):
    kl, vq = refs[0:4], refs[4:8]
    inverse_ref, key_ref, shrunk_ref, before_ref, state_ref, query_ref, core_ref = refs[8:]
    rank = rank_ref[0]
    row, col = iotas(n)
    tri = (row >= col).astype(BF16)
    every = range(4 * nh)
    at = [(i // 4, i % 4) for i in every]
    value = chunks_of(vq, rank, slice(0, n), nh, n)
    query = [x.astype(F32) for x in chunks_of(vq, rank, slice(n, 2 * n), nh, n)]
    cum = [dot1(tri, l) for l in chunks_of(kl, rank, slice(n, 2 * n), nh, n)]
    mid = [c[n // 2 - 1 : n // 2] for c in cum]
    solved = [split(dot2(load_split(inverse_ref, at[i]), value[i])) for i in every]
    grown = [query[i] * jnp.exp(cum[i] - mid[i]) for i in every]
    mix = [
        split(jnp.where(row >= col, dot3(split(grown[i]), load_split(shrunk_ref, at[i]), ROWS), 0.0))
        for i in every
    ]
    query = [split(grown[i] * jnp.exp(mid[i]) - dot3(mix[i], load_split(key_ref, at[i]))) for i in every]
    core = [dot3(mix[i], solved[i]) for i in every]
    for i in every:
        h, c = at[i]
        if c == 0:
            core_ref[h, c] = core[i]
            query_ref[h, c, :, 0:n] = query[i][0]
            query_ref[h, c, :, n : 2 * n] = query[i][1]
        else:
            core_ref[h, c] = core[i] + dot3(query[i], load_split(state_ref, (h, c - 1)))
            store_split(query_ref, (h, c), dot3(query[i], load_split(before_ref, (h, c - 1))))


def finish_kernel(nh, n, rank_ref, start_ref, query_ref, core_ref, gain_ref, out_ref):
    for h in range(nh):
        start = start_ref[h]
        for c in range(4):
            core = core_ref[h, c] + dot2(load_split(query_ref, (h, c)), start)
            scale = lax.rsqrt(jnp.mean(core * core, axis=-1, keepdims=True) + 1e-05)
            gain = gain_ref[:, h * n : (h + 1) * n]
            out_ref[c * n : (c + 1) * n, h * n : (h + 1) * n] = (core * scale * gain).astype(BF16)


def product_kernel(offsets, width, n, rank_ref, *refs):
    normed, weights = refs[:4], refs[4 : 4 + len(offsets)]
    outs, scratch = refs[4 + len(offsets) : -1], refs[-1]
    rank = rank_ref[0]
    for w, offset in zip(weights, offsets):
        total = None
        for x in range(4):
            at = pl.multiple_of((rank ^ x) * width, width)
            term = dot1(w[:, pl.ds(at, width)], normed[x][...], ROWS)
            total = term if total is None else total + term
        scratch[offset : offset + w.shape[0], :] = total
    for x in range(4):
        at = pl.multiple_of((rank ^ x) * n, n)
        outs[x][...] = scratch[:, pl.ds(at, n)].astype(BF16)


def assemble_kernel(groups, cols, n, place_ref, *refs):
    pieces, out_ref, wide, tall = refs[:4], refs[4], refs[5], refs[6]
    rank, group = place_ref[0], place_ref[1]
    for x in range(4):
        wide[...] = pieces[x][...].astype(F32)
        for g in range(groups):
            there = lax.rem(group + groups - g, groups) * QUAD + (rank ^ x)
            at = pl.multiple_of(there * cols, 8)
            tall[pl.ds(at, cols), :] = wide[g * cols : (g + 1) * cols, :]
    for j in range(tall.shape[0] // n):
        out_ref[:, j * n : (j + 1) * n] = tall[j * n : (j + 1) * n, :].T.astype(BF16)


def per_device(q, k, v, l, strength, gain, weight):
    q, k, v, l, strength, weight = (a[0] for a in (q, k, v, l, strength, weight))
    tok, hk = q.shape
    heads = strength.shape[0]
    dk = hk // heads
    seq = lax.axis_size("seq")
    sections = lax.axis_size("section")
    groups = seq // QUAD
    width = hk // QUAD
    hq = heads // QUAD
    cols = weight.shape[1]
    position = lax.axis_index("seq")
    rank = (position & (QUAD - 1)).astype(jnp.int32)
    group = (position // QUAD).astype(jnp.int32)
    rank1 = rank.reshape(1)
    smem = pl.BlockSpec(memory_space=pltpu.SMEM)
    anywhere = pl.BlockSpec(memory_space=pltpu.HBM)

    def call(kernel, name, limit=16, **kw):
        params = pltpu.CompilerParams(vmem_limit_bytes=limit << 20)
        return pl.pallas_call(kernel, name=name, compiler_params=params, **kw)

    def shape(dims, dtype):
        return jax.ShapeDtypeStruct(dims, dtype)

    def in_hbm(value):
        return pltpu.with_memory_space_constraint(value, pltpu.HBM)

    def near(value, x):
        return lax.ppermute(value, "seq", [(i, i ^ x) for i in range(seq)])

    def full(dims):
        return pl.BlockSpec(dims, lambda *_: (0,) * len(dims))

    kl = call(
        functools.partial(pack_kl, tok, width, dk),
        "pack_kl",
        in_specs=[smem, anywhere, anywhere, pl.BlockSpec(memory_space=pltpu.VMEM)],
        out_shape=[shape((2 * tok + 16, width), BF16)] * 4,
        scratch_shapes=[pltpu.SemaphoreType.DMA((8,))],
    )(rank1, in_hbm(k), in_hbm(l), strength)
    vq = call(
        functools.partial(pack_vq, tok, width),
        "pack_vq",
        in_specs=[smem, anywhere, anywhere],
        out_shape=[shape((2 * tok, width), BF16)] * 4,
        scratch_shapes=[pltpu.SemaphoreType.DMA((8,))],
    )(rank1, in_hbm(v), in_hbm(q))
    kl = [kl[0]] + [near(kl[x], x) for x in range(1, 4)]
    weight = weight.T
    cuts = [0, *(cols * share // 24 // 8 * 8 for share in SHARES), cols]
    weights, offsets = [weight], [0]

    def send_part(i, *after):
        part, *_ = lax.optimization_barrier((weight[cuts[i] : cuts[i + 1]], *after))
        for g in range(1, groups):
            weights.append(lax.ppermute(part, "seq", [(j, (j + g * QUAD) % seq) for j in range(seq)]))
            offsets.append(g * cols + cuts[i])

    def wait_for(i, *values):
        at = slice(1 + i * (groups - 1), 1 + (i + 1) * (groups - 1))
        *values, parts = lax.optimization_barrier((*values, weights[at]))
        weights[at] = parts
        return values

    vq_1, vq_2, vq_3, *_ = lax.optimization_barrier((*vq[1:], kl[1], kl[2]))
    vq = [vq[0], near(vq_1, 1), near(vq_2, 2), near(vq_3, 3)]
    send_part(0, kl[1], kl[2])

    two = 2
    kl_spec = pl.BlockSpec((2 * tok + 16, two * dk), lambda h: (0, h))
    vq_spec = pl.BlockSpec((2 * tok, two * dk), lambda h: (0, h))
    v_spec = pl.BlockSpec((tok, hq * dk), lambda h: (0, h))
    pair = lambda count: pl.BlockSpec((two, count, tok, 2 * dk), lambda h: (h, 0, 0, 0))
    pairs = lambda count: shape((hq, count, tok, 2 * dk), BF16)
    more = groups > 2
    inverse, offset, key, shrunk, maps, before, *whole_map = call(
        functools.partial(maps_kernel, two, tok, more),
        "maps",
        limit=32,
        grid=(hq // two,),
        in_specs=[smem] + [kl_spec] * 4,
        out_specs=[pair(4)] * 5 + [pair(3)] + [pl.BlockSpec((two, dk, dk), lambda h: (h, 0, 0))] * more,
        out_shape=[pairs(4)] * 5 + [pairs(3)] + [shape((hq, dk, dk), F32)] * more,
    )(rank1, *kl)
    all4 = lambda count: full((hq, count, tok, 2 * dk))
    states, total = call(
        functools.partial(states_kernel, hq, tok),
        "states",
        limit=24,
        grid=(1,),
        in_specs=[smem] + [v_spec] * 4 + [all4(4)] * 2,
        out_specs=[all4(3), full((hq, dk, dk))],
        out_shape=[pairs(3), shape((hq, dk, dk), F32 if more else BF16)],
    )(rank1, *vq, offset, maps)

    onward = [(i, i + QUAD) for i in range(seq - QUAD)]
    start = lax.ppermute(total, "seq", onward)
    for _ in range(groups - 2):
        state = jnp.einsum("hde,hef->hdf", whole_map[0], start, precision=lax.Precision.HIGHEST)
        start = lax.ppermute(state + total, "seq", onward)
    start = start.astype(BF16)
    query, core = call(
        functools.partial(local_kernel, two, tok),
        "local",
        limit=32,
        grid=(hq // two,),
        in_specs=[smem] + [kl_spec] * 4 + [vq_spec] * 4 + [pair(4)] * 3 + [pair(3)] * 2,
        out_specs=[pair(4), pl.BlockSpec((two, 4, tok, dk), lambda h: (h, 0, 0, 0))],
        out_shape=[pairs(4), shape((hq, 4, tok, dk), F32)],
    )(rank1, *kl, *vq, inverse, key, shrunk, before, states)
    start, core = lax.optimization_barrier((start, core))
    start, core = wait_for(0, start, core)
    send_part(1, start)
    normed = call(
        functools.partial(finish_kernel, hq, tok),
        "finish",
        grid_spec=pltpu.PrefetchScalarGridSpec(
            num_scalar_prefetch=1,
            grid=(1,),
            in_specs=[
                full((hq, dk, dk)),
                all4(4),
                full((hq, 4, tok, dk)),
                pl.BlockSpec((1, width), lambda h, place: (0, place[0])),
            ],
            out_specs=full((QUAD * tok, width)),
        ),
        out_shape=shape((QUAD * tok, width), BF16),
    )(rank1, start, query, core, gain)

    beside, across = near(normed, 1), near(normed, 2)
    normed = [normed, beside, across, near(across, 1)]
    pieces = call(
        functools.partial(product_kernel, offsets, width, tok),
        "product",
        limit=24,
        grid=(1,),
        in_specs=[smem] + [full((QUAD * tok, width))] * 4 + [full(w.shape) for w in weights],
        out_specs=[full((groups * cols, tok))] * 4,
        out_shape=[shape((groups * cols, tok), BF16)] * 4,
        scratch_shapes=[pltpu.VMEM((groups * cols, QUAD * tok), F32)],
    )(rank1, *normed, *weights)

    got = []
    for x in range(4):
        relay = [
            (i * sections + s, (i ^ x) * sections + (s + 1) % sections)
            for i in range(seq)
            for s in range(sections)
        ]
        got.append(lax.ppermute(pieces[x], ("seq", "section"), relay))
    out = call(
        functools.partial(assemble_kernel, groups, cols, tok),
        "assemble",
        grid=(1,),
        in_specs=[smem] + [full((groups * cols, tok))] * 4,
        out_specs=full((tok, seq * cols)),
        out_shape=shape((tok, seq * cols), BF16),
        scratch_shapes=[pltpu.VMEM((groups * cols, tok), F32), pltpu.VMEM((seq * cols, tok), F32)],
    )(jnp.stack([rank, group]), *got)
    return out[None]


def solution(mesh):
    in_specs = (
        P("section", "seq", None),
        P("section", "seq", None),
        P("section", "seq", None),
        P("section", "seq", None),
        P("section", None, "seq"),
        P("section", None),
        P("section", None, "seq"),
    )
    out_specs = P("section", "seq", None)
    return jax.shard_map(
        per_device, mesh=mesh, in_specs=in_specs, out_specs=out_specs, check_vma=False
    )
```

```python
import functools

import jax
import jax.numpy as jnp
from jax import lax
from jax.experimental import pallas as pl
from jax.experimental.pallas import tpu as pltpu
from jax.sharding import PartitionSpec as P

F32 = jnp.float32
BF16 = jnp.bfloat16
QUAD = 4
SHARES = (8,)
ROWS = ((1,), (1,))


def split(a):
    high = a.astype(BF16)
    return high, (a - high.astype(F32)).astype(BF16)


def store_split(ref, at, a):
    high, low = split(a)
    n = a.shape[1]
    ref[(*at, slice(None), slice(0, n))] = high
    ref[(*at, slice(None), slice(n, 2 * n))] = low


def load_split(ref, at):
    both = ref[at]
    n = both.shape[1] // 2
    return both[:, :n], both[:, n:]


def dot1(a, b, dims=((1,), (0,))):
    return lax.dot_general(a, b, (dims, ((), ())), preferred_element_type=F32)


def dot2(a, b, dims=((1,), (0,))):
    return dot1(a[0], b, dims) + dot1(a[1], b, dims)


def dot3(a, b, dims=((1,), (0,))):
    return dot1(a[0], b[0], dims) + dot1(a[0], b[1], dims) + dot1(a[1], b[0], dims)


def iotas(n):
    row = lax.broadcasted_iota(jnp.int32, (n, n), 0)
    col = lax.broadcasted_iota(jnp.int32, (n, n), 1)
    return row, col


def unit_lower_inverses(stricts, row, col):
    n = stricts[0].shape[0]
    eye = (row == col).astype(F32)
    inverses = None
    size = 1
    while size < n:
        shift = size.bit_length() - 1
        joins = ((row >> (shift + 1)) == (col >> (shift + 1))) & ((row >> shift) > (col >> shift))
        below = [jnp.where(joins, s, 0.0) for s in stricts]
        if size == 1:
            inverses = [eye - b for b in below]
        else:
            parts = [split(i) for i in inverses]
            inner = [split(dot3(split(b), p)) for b, p in zip(below, parts)]
            outer = [dot3(p, t) for p, t in zip(parts, inner)]
            inverses = [i - o for i, o in zip(inverses, outer)]
        size *= 2
    return inverses


def pick(pieces, rank):
    p = list(pieces)
    one = (rank & 1) == 1
    two = (rank & 2) == 2
    p = [jnp.where(one, p[x ^ 1], p[x]) for x in range(4)]
    return [jnp.where(two, p[x ^ 2], p[x]) for x in range(4)]


def pack_kl(tok, width, dk, rank_ref, k_ref, l_ref, b_ref, *refs):
    outs, sem = refs[:4], refs[4]
    rank = rank_ref[0]
    heads = width // dk
    copies = []
    for x in range(4):
        at = pl.multiple_of((rank ^ x) * width, width)
        for i, source in enumerate((k_ref, l_ref)):
            copy = pltpu.make_async_copy(
                source.at[:, pl.ds(at, width)], outs[x].at[i * tok : (i + 1) * tok, :], sem.at[2 * x + i]
            )
            copy.start()
            copies.append(copy)
    for x in range(4):
        for h in range(heads):
            strength = b_ref[pl.ds((rank ^ x) * heads + h, 1), :]
            first, rest = split(strength)
            second, third = split(strength - first.astype(F32))
            rows = jnp.concatenate(
                [first.astype(F32), second.astype(F32), third.astype(F32), jnp.zeros((13, tok), F32)], axis=0
            )
            outs[x][2 * tok : 2 * tok + 16, h * dk : (h + 1) * dk] = rows.astype(BF16)
    for copy in copies:
        copy.wait()


def pack_vq(tok, width, rank_ref, v_ref, q_ref, *refs):
    outs, sem = refs[:8], refs[8]
    rank = rank_ref[0]
    copies = []
    for i, source in enumerate((v_ref, q_ref)):
        for x in range(4):
            at = pl.multiple_of((rank ^ x) * width, width)
            copy = pltpu.make_async_copy(source.at[:, pl.ds(at, width)], outs[4 * i + x], sem.at[4 * i + x])
            copy.start()
            copies.append(copy)
    for copy in copies:
        copy.wait()


def chunks_of(refs, rank, rows, nh, dk):
    out = []
    for h in range(nh):
        out += pick([r[rows, h * dk : (h + 1) * dk] for r in refs], rank)
    return out


def maps_kernel(nh, n, more, rank_ref, *refs):
    kl = refs[0:4]
    inverse_ref, offset_ref, key_ref, shrunk_ref, map_ref, before_ref = refs[4:10]
    rank = rank_ref[0]
    row, col = iotas(n)
    diag = row == col
    tri = (row >= col).astype(BF16)
    every = range(4 * nh)
    at = [(i // 4, i % 4) for i in every]
    bs = [b.astype(F32) for b in chunks_of(kl, rank, slice(2 * n, 2 * n + 16), nh, n)]
    bs = [b[0:1] + b[1:2] + b[2:3] for b in bs]
    strength = [jnp.sum(jnp.where(diag, b, 0.0), axis=1, keepdims=True) for b in bs]
    key = [k.astype(F32) for k in chunks_of(kl, rank, slice(0, n), nh, n)]
    key = [k * lax.rsqrt(jnp.sum(k * k, axis=-1, keepdims=True) + 1e-06) for k in key]
    cum = [dot1(tri, l) for l in chunks_of(kl, rank, slice(n, 2 * n), nh, n)]
    mid = [c[n // 2 - 1 : n // 2] for c in cum]
    end = [c[n - 1 : n] for c in cum]
    grown = [split(key[i] * jnp.exp(cum[i] - mid[i])) for i in every]
    shrunk = [key[i] * jnp.exp(mid[i] - cum[i]) * strength[i] for i in every]
    shrunk_s = [split(s) for s in shrunk]
    strict = [jnp.where(row > col, dot3(grown[i], shrunk_s[i], ROWS), 0.0) for i in every]
    inverse = [split(x) for x in unit_lower_inverses(strict, row, col)]
    solved = [split(dot3(inverse[i], grown[i]) * jnp.exp(mid[i])) for i in every]
    end_keys = [split((shrunk[i] * jnp.exp(end[i] - mid[i])).T) for i in every]
    end_col = [jnp.sum(jnp.where(diag, jnp.exp(e), 0.0), axis=1, keepdims=True) for e in end]
    step = [jnp.where(diag, end_col[i], 0.0) - dot3(end_keys[i], solved[i]) for i in every]
    step_s = [split(s) for s in step]
    for i in every:
        for ref, value in ((inverse_ref, inverse[i]), (key_ref, solved[i]), (shrunk_ref, shrunk_s[i]), (map_ref, step_s[i])):
            ref[(*at[i], slice(None), slice(0, n))] = value[0]
            ref[(*at[i], slice(None), slice(n, 2 * n))] = value[1]
        store_split(offset_ref, at[i], dot3(end_keys[i], inverse[i]))
    before = [step[4 * h] for h in range(nh)]
    for c in range(1, 4):
        for h in range(nh):
            store_split(before_ref, (h, c - 1), before[h])
            if c < 3 or more:
                before[h] = dot3(step_s[4 * h + c], split(before[h]))
    if more:
        for h in range(nh):
            refs[10][h] = before[h]


def states_kernel(nh, n, rank_ref, *refs):
    v = refs[0:4]
    offset_ref, map_ref, state_ref, total_ref = refs[4:]
    value = chunks_of(v, rank_ref[0], slice(0, n), nh, n)
    offset = [dot2(load_split(offset_ref, (i // 4, i % 4)), value[i]) for i in range(4 * nh)]
    state = [offset[4 * h] for h in range(nh)]
    for c in range(1, 4):
        parts = [split(s) for s in state]
        for h in range(nh):
            state_ref[h, c - 1, :, 0:n] = parts[h][0]
            state_ref[h, c - 1, :, n : 2 * n] = parts[h][1]
        state = [dot3(load_split(map_ref, (h, c)), parts[h]) + offset[4 * h + c] for h in range(nh)]
    for h in range(nh):
        total_ref[h] = state[h].astype(total_ref.dtype)


def local_kernel(nh, n, rank_ref, *refs):
    kl, v, q = refs[0:4], refs[4:8], refs[8:12]
    inverse_ref, key_ref, shrunk_ref, before_ref, state_ref, query_ref, core_ref = refs[12:]
    rank = rank_ref[0]
    row, col = iotas(n)
    tri = (row >= col).astype(BF16)
    every = range(4 * nh)
    at = [(i // 4, i % 4) for i in every]
    value = chunks_of(v, rank, slice(0, n), nh, n)
    query = [x.astype(F32) for x in chunks_of(q, rank, slice(0, n), nh, n)]
    cum = [dot1(tri, l) for l in chunks_of(kl, rank, slice(n, 2 * n), nh, n)]
    mid = [c[n // 2 - 1 : n // 2] for c in cum]
    solved = [split(dot2(load_split(inverse_ref, at[i]), value[i])) for i in every]
    grown = [query[i] * jnp.exp(cum[i] - mid[i]) for i in every]
    mix = [
        split(jnp.where(row >= col, dot3(split(grown[i]), load_split(shrunk_ref, at[i]), ROWS), 0.0))
        for i in every
    ]
    query = [split(grown[i] * jnp.exp(mid[i]) - dot3(mix[i], load_split(key_ref, at[i]))) for i in every]
    core = [dot3(mix[i], solved[i]) for i in every]
    for i in every:
        h, c = at[i]
        if c == 0:
            core_ref[h, c] = core[i]
            query_ref[h, c, :, 0:n] = query[i][0]
            query_ref[h, c, :, n : 2 * n] = query[i][1]
        else:
            core_ref[h, c] = core[i] + dot3(query[i], load_split(state_ref, (h, c - 1)))
            store_split(query_ref, (h, c), dot3(query[i], load_split(before_ref, (h, c - 1))))


def finish_kernel(nh, n, rank_ref, start_ref, query_ref, core_ref, gain_ref, out_ref):
    for h in range(nh):
        start = start_ref[h]
        for c in range(4):
            core = core_ref[h, c] + dot2(load_split(query_ref, (h, c)), start)
            scale = lax.rsqrt(jnp.mean(core * core, axis=-1, keepdims=True) + 1e-05)
            gain = gain_ref[:, h * n : (h + 1) * n]
            out_ref[c * n : (c + 1) * n, h * n : (h + 1) * n] = (core * scale * gain).astype(BF16)


def product_kernel(offsets, width, n, rank_ref, *refs):
    normed, weights = refs[:4], refs[4 : 4 + len(offsets)]
    outs, scratch = refs[4 + len(offsets) : -1], refs[-1]
    rank = rank_ref[0]
    for w, offset in zip(weights, offsets):
        total = None
        for x in range(4):
            at = pl.multiple_of((rank ^ x) * width, width)
            term = dot1(w[:, pl.ds(at, width)], normed[x][...], ROWS)
            total = term if total is None else total + term
        scratch[offset : offset + w.shape[0], :] = total
    for x in range(4):
        at = pl.multiple_of((rank ^ x) * n, n)
        outs[x][...] = scratch[:, pl.ds(at, n)].astype(BF16)


def assemble_kernel(groups, cols, n, place_ref, *refs):
    pieces, out_ref, wide, tall = refs[:4], refs[4], refs[5], refs[6]
    rank, group = place_ref[0], place_ref[1]
    for x in range(4):
        wide[...] = pieces[x][...].astype(F32)
        for g in range(groups):
            there = lax.rem(group + groups - g, groups) * QUAD + (rank ^ x)
            at = pl.multiple_of(there * cols, 8)
            tall[pl.ds(at, cols), :] = wide[g * cols : (g + 1) * cols, :]
    for j in range(tall.shape[0] // n):
        out_ref[:, j * n : (j + 1) * n] = tall[j * n : (j + 1) * n, :].T.astype(BF16)


def per_device(q, k, v, l, strength, gain, weight):
    q, k, v, l, strength, weight = (a[0] for a in (q, k, v, l, strength, weight))
    tok, hk = q.shape
    heads = strength.shape[0]
    dk = hk // heads
    seq = lax.axis_size("seq")
    sections = lax.axis_size("section")
    groups = seq // QUAD
    width = hk // QUAD
    hq = heads // QUAD
    cols = weight.shape[1]
    position = lax.axis_index("seq")
    rank = (position & (QUAD - 1)).astype(jnp.int32)
    group = (position // QUAD).astype(jnp.int32)
    rank1 = rank.reshape(1)
    smem = pl.BlockSpec(memory_space=pltpu.SMEM)
    anywhere = pl.BlockSpec(memory_space=pltpu.HBM)

    def call(kernel, name, limit=16, **kw):
        params = pltpu.CompilerParams(vmem_limit_bytes=limit << 20)
        return pl.pallas_call(kernel, name=name, compiler_params=params, **kw)

    def shape(dims, dtype):
        return jax.ShapeDtypeStruct(dims, dtype)

    def in_hbm(value):
        return pltpu.with_memory_space_constraint(value, pltpu.HBM)

    def near(value, x):
        return lax.ppermute(value, "seq", [(i, i ^ x) for i in range(seq)])

    def full(dims):
        return pl.BlockSpec(dims, lambda *_: (0,) * len(dims))

    kl = call(
        functools.partial(pack_kl, tok, width, dk),
        "pack_kl",
        in_specs=[smem, anywhere, anywhere, pl.BlockSpec(memory_space=pltpu.VMEM)],
        out_shape=[shape((2 * tok + 16, width), BF16)] * 4,
        scratch_shapes=[pltpu.SemaphoreType.DMA((8,))],
    )(rank1, in_hbm(k), in_hbm(l), strength)
    vq = call(
        functools.partial(pack_vq, tok, width),
        "pack_vq",
        in_specs=[smem, anywhere, anywhere],
        out_shape=[shape((tok, width), BF16)] * 8,
        scratch_shapes=[pltpu.SemaphoreType.DMA((8,))],
    )(rank1, in_hbm(v), in_hbm(q))
    kl = [kl[0]] + [near(kl[x], x) for x in range(1, 4)]
    weight = weight.T
    cuts = [0, *(cols * share // 24 // 8 * 8 for share in SHARES), cols]
    weights, offsets = [weight], [0]

    def send_part(i, *after):
        part, *_ = lax.optimization_barrier((weight[cuts[i] : cuts[i + 1]], *after))
        for g in range(1, groups):
            weights.append(lax.ppermute(part, "seq", [(j, (j + g * QUAD) % seq) for j in range(seq)]))
            offsets.append(g * cols + cuts[i])

    def wait_for(i, *values):
        at = slice(1 + i * (groups - 1), 1 + (i + 1) * (groups - 1))
        *values, parts = lax.optimization_barrier((*values, weights[at]))
        weights[at] = parts
        return values

    v_1, v_2, v_3, *_ = lax.optimization_barrier((*vq[1:4], kl[1], kl[2]))
    v_all = [vq[0], near(v_1, 1), near(v_2, 2), near(v_3, 3)]
    send_part(0, kl[1], kl[2])

    two = 2
    kl_spec = pl.BlockSpec((2 * tok + 16, two * dk), lambda h: (0, h))
    vq_spec = pl.BlockSpec((tok, two * dk), lambda h: (0, h))
    v_spec = pl.BlockSpec((tok, hq * dk), lambda h: (0, h))
    pair = lambda count: pl.BlockSpec((two, count, tok, 2 * dk), lambda h: (h, 0, 0, 0))
    pairs = lambda count: shape((hq, count, tok, 2 * dk), BF16)
    more = groups > 2
    inverse, offset, key, shrunk, maps, before, *whole_map = call(
        functools.partial(maps_kernel, two, tok, more),
        "maps",
        limit=32,
        grid=(hq // two,),
        in_specs=[smem] + [kl_spec] * 4,
        out_specs=[pair(4)] * 5 + [pair(3)] + [pl.BlockSpec((two, dk, dk), lambda h: (h, 0, 0))] * more,
        out_shape=[pairs(4)] * 5 + [pairs(3)] + [shape((hq, dk, dk), F32)] * more,
    )(rank1, *kl)
    q_1, q_2, q_3, *_ = lax.optimization_barrier((*vq[5:], inverse))
    q_all = [vq[4], near(q_1, 1), near(q_2, 2), near(q_3, 3)]
    all4 = lambda count: full((hq, count, tok, 2 * dk))
    states, total = call(
        functools.partial(states_kernel, hq, tok),
        "states",
        limit=24,
        grid=(1,),
        in_specs=[smem] + [v_spec] * 4 + [all4(4)] * 2,
        out_specs=[all4(3), full((hq, dk, dk))],
        out_shape=[pairs(3), shape((hq, dk, dk), F32 if more else BF16)],
    )(rank1, *v_all, offset, maps)

    onward = [(i, i + QUAD) for i in range(seq - QUAD)]
    start = lax.ppermute(total, "seq", onward)
    for _ in range(groups - 2):
        state = jnp.einsum("hde,hef->hdf", whole_map[0], start, precision=lax.Precision.HIGHEST)
        start = lax.ppermute(state + total, "seq", onward)
    start = start.astype(BF16)
    query, core = call(
        functools.partial(local_kernel, two, tok),
        "local",
        limit=32,
        grid=(hq // two,),
        in_specs=[smem] + [kl_spec] * 4 + [vq_spec] * 8 + [pair(4)] * 3 + [pair(3)] * 2,
        out_specs=[pair(4), pl.BlockSpec((two, 4, tok, dk), lambda h: (h, 0, 0, 0))],
        out_shape=[pairs(4), shape((hq, 4, tok, dk), F32)],
    )(rank1, *kl, *v_all, *q_all, inverse, key, shrunk, before, states)
    start, core = lax.optimization_barrier((start, core))
    start, core = wait_for(0, start, core)
    send_part(1, start)
    normed = call(
        functools.partial(finish_kernel, hq, tok),
        "finish",
        grid_spec=pltpu.PrefetchScalarGridSpec(
            num_scalar_prefetch=1,
            grid=(1,),
            in_specs=[
                full((hq, dk, dk)),
                all4(4),
                full((hq, 4, tok, dk)),
                pl.BlockSpec((1, width), lambda h, place: (0, place[0])),
            ],
            out_specs=full((QUAD * tok, width)),
        ),
        out_shape=shape((QUAD * tok, width), BF16),
    )(rank1, start, query, core, gain)

    beside, across = near(normed, 1), near(normed, 2)
    normed = [normed, beside, across, near(across, 1)]
    pieces = call(
        functools.partial(product_kernel, offsets, width, tok),
        "product",
        limit=24,
        grid=(1,),
        in_specs=[smem] + [full((QUAD * tok, width))] * 4 + [full(w.shape) for w in weights],
        out_specs=[full((groups * cols, tok))] * 4,
        out_shape=[shape((groups * cols, tok), BF16)] * 4,
        scratch_shapes=[pltpu.VMEM((groups * cols, QUAD * tok), F32)],
    )(rank1, *normed, *weights)

    got = []
    for x in range(4):
        relay = [
            (i * sections + s, (i ^ x) * sections + (s + 1) % sections)
            for i in range(seq)
            for s in range(sections)
        ]
        got.append(lax.ppermute(pieces[x], ("seq", "section"), relay))
    out = call(
        functools.partial(assemble_kernel, groups, cols, tok),
        "assemble",
        grid=(1,),
        in_specs=[smem] + [full((groups * cols, tok))] * 4,
        out_specs=full((tok, seq * cols)),
        out_shape=shape((tok, seq * cols), BF16),
        scratch_shapes=[pltpu.VMEM((groups * cols, tok), F32), pltpu.VMEM((seq * cols, tok), F32)],
    )(jnp.stack([rank, group]), *got)
    return out[None]


def solution(mesh):
    in_specs = (
        P("section", "seq", None),
        P("section", "seq", None),
        P("section", "seq", None),
        P("section", "seq", None),
        P("section", None, "seq"),
        P("section", None),
        P("section", None, "seq"),
    )
    out_specs = P("section", "seq", None)
    return jax.shard_map(
        per_device, mesh=mesh, in_specs=in_specs, out_specs=out_specs, check_vma=False
    )
```
